256 devices in a mesh: mesh: 32 (over x_lo, z, core), mem: 8 (over y, x_hi).
Axes of the slice: x: 4 (x_hi: 2, x_lo: 2; x = x_hi * 2 + x_lo), y: 4, z: 8, core: 2. Of those that a mesh axis runs over, the one named last changes fastest.
Arguments:
- perturbations: bfloat16 [12288, 16384], P('mem', 'mesh')
- node_coord: int32 [16384], P('mesh'), may hold values from 0 to 65535, as said below
- threshold_level: int32 [16384], P('mesh'), may hold values from 0 to 4
Outputs:
- band_cov: float32 [16384, 2048], P(('mesh', 'mem'))
The draws below stay inside these ranges and needn't reach their ends.
Inputs may be any that keep to these rules, and one draw needn't show every extreme that they name: node_coord[n] lies in 4 n to 4 n + 3; node 0 has 0 and the last node 65535.
All inputs are finite; a program needn't handle non-finite values.
Results may differ from the reference program's by a relative error of at most 0.0003.
Values may be sent and summed in bfloat16 or wider, within the bound.
A program may use at most 64 MiB of HBM per device.

```python
import jax
import jax.numpy as jnp
from jax import lax

NB = 512
SHIFTS = 3
FACTORS = 8
NODES = 16384
MEMBERS = 12288
WIDE = 2048
TAPER_HALF = 6144


def draw_perturbations(key, part):
    key_noise = jax.random.fold_in(key, 11)
    key_modes = jax.random.fold_in(key, 12)
    key_load = jax.random.fold_in(key, 13)
    noise = jax.random.normal(key_noise, (MEMBERS, NODES), jnp.float32)
    modes = jax.random.normal(key_modes, (MEMBERS, FACTORS), jnp.float32)
    loads = 0.25 * jax.random.normal(key_load, (FACTORS, NODES), jnp.float32)
    values = noise + jnp.dot(modes, loads, precision=lax.Precision.HIGHEST)
    return values.astype(jnp.bfloat16)


def draw_node_coord(key, part):
    jitter = jax.random.randint(jax.random.fold_in(key, 21), (NODES,), 0, 4)
    jitter = jitter.at[0].set(0).at[NODES - 1].set(3)
    return (4 * jnp.arange(NODES, dtype=jnp.int32) + jitter).astype(jnp.int32)


def set_ends(entries, key, smallest, largest):
    shape = entries.shape
    spot = [jax.random.randint(jax.random.fold_in(key, axis), (), 0, shape[axis]) for axis in range(len(shape))]
    entries = entries.at[tuple(spot)].set(smallest)
    longest = shape.index(max(shape))
    spot[longest] = (spot[longest] + 1) % shape[longest]
    return entries.at[tuple(spot)].set(largest)


def setup_inputs(seed: int = 0) -> dict:
    seeds = jax.random.split(jax.random.key(seed), 4)
    perturbations = draw_perturbations(jax.random.fold_in(seeds[3], 71), 0)
    node_coord = draw_node_coord(jax.random.fold_in(seeds[3], 71), 0)
    threshold_level = set_ends(jax.random.randint(seeds[2], (NODES,), 0, 5), jax.random.fold_in(seeds[2], 1), 0, 4).astype(jnp.int32)
    return {"perturbations": perturbations, "node_coord": node_coord, "threshold_level": threshold_level}


def gc_taper(radius):
    near = -0.25 * radius ** 5 + 0.5 * radius ** 4 + 0.625 * radius ** 3 - (5.0 / 3.0) * radius ** 2 + 1.0
    safe = jnp.maximum(radius, 1.0)
    far = safe ** 5 / 12.0 - 0.5 * safe ** 4 + 0.625 * safe ** 3 + (5.0 / 3.0) * safe ** 2 - 5.0 * safe + 4.0 - 2.0 / (3.0 * safe)
    return jnp.where(radius <= 1.0, near, jnp.where(radius <= 2.0, far, 0.0))


def reference(perturbations, node_coord, threshold_level):
    parts = NODES // NB
    period = 4 * NODES
    whole = perturbations.astype(jnp.float32)

    def one_part(index):
        own = lax.dynamic_slice_in_dim(whole, (index * NB).astype(jnp.int32), NB, 1)
        own_coord = lax.dynamic_slice_in_dim(node_coord, (index * NB).astype(jnp.int32), NB, 0)
        own_level = lax.dynamic_slice_in_dim(threshold_level, (index * NB).astype(jnp.int32), NB, 0)
        level = (0.05 * own_level.astype(jnp.float32))[:, None]
        columns = []
        coords = []
        for step in range(SHIFTS + 1):
            start = (((index + step) % parts) * NB).astype(jnp.int32)
            columns.append(lax.dynamic_slice_in_dim(whole, start, NB, 1))
            coords.append(lax.dynamic_slice_in_dim(node_coord, start, NB, 0))
        columns = jnp.concatenate(columns, axis=1)
        coords = jnp.concatenate(coords, axis=0)
        raw = lax.dot_general(own, columns, (((0,), (0,)), ((), ())), precision=lax.Precision.HIGHEST, preferred_element_type=jnp.float32)
        cov = raw / jnp.float32(MEMBERS - 1)
        gap = jnp.mod(coords[None, :] - own_coord[:, None], period)
        dist = jnp.minimum(gap, period - gap).astype(jnp.float32)
        taper = gc_taper(dist / jnp.float32(TAPER_HALF))
        tapered = taper * cov
        return tapered - jnp.clip(tapered, -level, level)

    blocks = lax.map(one_part, jnp.arange(parts, dtype=jnp.int32))
    return blocks.reshape(NODES, WIDE)
```

```python
import functools

import jax
import jax.numpy as jnp
from jax import lax
from jax.experimental import pallas as pl
from jax.experimental.pallas import tpu as pltpu
from jax.sharding import PartitionSpec as P

MESH = pl.DeviceIdType.MESH
LANES = 128
STEPS = 32000.0
F32 = jnp.float32


def gc_taper(radius):
    r2 = radius * radius
    r3 = r2 * radius
    near = r3 * (0.625 + radius * (0.5 - 0.25 * radius)) - (5.0 / 3.0) * r2 + 1.0
    safe = jnp.maximum(radius, 1.0)
    s2 = safe * safe
    s3 = s2 * safe
    far = s3 * (0.625 + safe * (safe / 12.0 - 0.5)) + (5.0 / 3.0) * s2 - 5.0 * safe + 4.0 - 2.0 / (3.0 * safe)
    return jnp.where(radius <= 1.0, near, jnp.where(radius <= 2.0, far, 0.0))


def encode(blocks, store):
    top = functools.reduce(jnp.maximum, [jnp.max(jnp.abs(b), axis=0, keepdims=True) for b in blocks])
    power = jnp.ceil(jnp.log2(jnp.maximum(top, 1.2e-38)))
    half = jnp.floor(0.5 * power)
    one, two = jnp.exp2(-half), jnp.exp2(half - power) * STEPS
    at = 0
    for b in blocks:
        rows = b.shape[0]
        store(at, rows, jnp.round((b * one) * two).astype(jnp.int32).astype(jnp.int16))
        at += rows
    store(at, 16, jnp.broadcast_to(power, (16, LANES)).astype(jnp.int32).astype(jnp.int16))


def scale_of(ref, rows):
    power = ref[pl.ds(rows, 16), :].astype(jnp.int32).astype(F32)[0:1]
    half = jnp.floor(0.5 * power)
    return jnp.exp2(half), jnp.exp2(power - half) / STEPS


def decode(ref, at, rows, scale):
    return (ref[pl.ds(at, rows), :].astype(jnp.int32).astype(F32) * scale[0]) * scale[1]


def kernel(
    members, parts, period, reach,
    x_ref, coord_ref, level_ref, out_ref,
    held, turned, coords, rowv, weight, own_e, own_l, keep_e, keep_l, split,
    ysend_e, yrecv_e, ysend_l, yrecv_l, fsend_e, frecv_e, fsend_l, frecv_l,
    own_sem, zs, zr, bs, br, us, ur, cs, cr, yse, yre, ysl, yrl, fse, fre, fsl, frl,
):
    p, m = lax.axis_index("mesh"), lax.axis_index("mem")
    core, y, h = lax.rem(p, 2), m // 2, lax.rem(m, 2)
    far = m + 1 - 2 * h
    sib = p + 1 - 2 * core

    def at(shift):
        return lax.rem(p + shift + parts, parts)

    def ring(d):
        return (p, lax.rem(m + 2 * d, 8))

    barrier = pltpu.get_barrier_semaphore()
    peers = [(at(s), m) for s in (-3, -2, -1, 1, 2, 3)] + [ring(d) for d in (1, 2, 3)]
    peers += [(p, far), (at(1), far), (at(-1), far)]
    for peer in peers:
        pl.semaphore_signal(barrier, inc=1, device_id=peer, device_id_type=MESH)
    pl.semaphore_wait(barrier, len(peers))

    def send(src, dst, ssem, rsem, to):
        return pltpu.make_async_remote_copy(
            src_ref=src, dst_ref=dst, send_sem=ssem, recv_sem=rsem, device_id=to, device_id_type=MESH
        )

    def columns(j):
        return pl.ds(pl.multiple_of(j * LANES, LANES), LANES)

    def down(j):
        c = pl.ds(j * LANES, LANES)
        return send(x_ref.at[:, c], held.at[2, :, c], zs.at[j], zr.at[j], (at(-2), m))

    beside = send(x_ref, held.at[1], bs, br, (sib, m))
    up = send(x_ref, held.at[3], us, ur, (at(1), m))
    notes = [send(coord_ref, coords.at[k], cs.at[k], cr.at[k], (at(-1 - k), m)) for k in range(3)]
    beside.start()
    down(0).start()

    @pl.when(core == 1)
    def _():
        up.start()

    for j in range(1, 4):
        down(j).start()
    for note in notes:
        note.start()
    mine = pltpu.make_async_copy(x_ref, held.at[0], own_sem)
    mine.start()
    mine.wait()

    def turn(slot, to):
        def body(q, carry):
            turned[q, to] = held[slot, :, columns(q)].T
            return carry

        lax.fori_loop(0, 4, body, 0)

    turn(0, 0)

    def e_blocks(row):
        full = jnp.dot(turned[row, 0], held[0], preferred_element_type=F32)
        return [full[:, k * LANES : (k + 1) * LANES] for k in range(4)]

    def y_e(d):
        return send(ysend_e.at[d - 1], yrecv_e.at[d - 1], yse.at[d - 1], yre.at[d - 1], ring(d))

    for d in (2, 1, 3):

        def put(a, n, v, d=d):
            ysend_e[d - 1, pl.ds(a, n), :] = v

        encode(e_blocks(lax.rem(y + d, 4)), put)
        y_e(d).start()
    for k, b in enumerate(e_blocks(y)):
        own_e[k] = b

    def as_rows(ref):
        line = ref[0:1, columns(y)].astype(F32)
        return jnp.broadcast_to(line, (LANES, LANES)).T

    for k, ref in enumerate((coord_ref, level_ref)):
        v = as_rows(ref)
        rowv[k, 0] = v[0:64]
        rowv[k, 1] = v[64:128]
    row = rowv[0, h]
    limit = 0.05 * rowv[1, h]
    for note in notes:
        note.wait_recv()
    for s in range(4):
        for j in range(4):
            c = pl.ds(j * LANES, LANES)
            col = (coord_ref[0:1, c] if s == 0 else coords[s - 1, 0:1, c]).astype(F32)
            gap = col - row
            gap = jnp.where(gap < 0.0, gap + period, gap)
            dist = jnp.minimum(gap, period - gap)
            weight[s, j] = gc_taper(dist / reach) * (1.0 / (members - 1.0))

    def finish(value, s, j):
        c = weight[s, j] * value
        out_ref[:, pl.ds(pl.multiple_of((s * 4 + j) * LANES, LANES), LANES)] = c - jnp.clip(c, -limit, limit)

    beside.wait_recv()
    turn(1, 1)

    f_e = send(fsend_e, frecv_e, fse, fre, (p, far))
    for d in (1, 2, 3):
        y_e(d).wait_recv()
    scales = [scale_of(yrecv_e.at[d], 512) for d in range(3)]
    theirs = []
    for k in range(4):
        total = own_e[k]
        for d in range(3):
            total = total + decode(yrecv_e.at[d], k * LANES, LANES, scales[d])
        split[0, 0] = total[0:64]
        split[0, 1] = total[64:128]
        keep_e[k] = split[0, h]
        theirs.append(split[0, 1 - h])

    def put_e(a, n, v):
        fsend_e[pl.ds(a, n), :] = v

    encode(theirs, put_e)
    f_e.start()

    @pl.when(core == 0)
    def _():
        up.wait_recv()
        turn(3, 2)

    f_e.wait_recv()
    scale = scale_of(frecv_e, 256)
    for k in range(4):
        finish(keep_e[k] + decode(frecv_e, k * 64, 64, scale), 0, k)

    lhs2, rhs2 = 1 + (1 - core), 2 * (1 - core)

    def l_blocks(row, j):
        c = pl.ds(j * LANES, LANES)
        pair = turned[row, 0:2].reshape(2 * LANES, members // 8)
        both = jnp.dot(pair, held[2, :, c], preferred_element_type=F32)
        third = jnp.dot(turned[row, lhs2], held[rhs2, :, c], preferred_element_type=F32)
        return [both[0:LANES], both[LANES:], third]

    def y_l(j, d):
        return send(ysend_l.at[j, d - 1], yrecv_l.at[j, d - 1], ysl.at[j, d - 1], yrl.at[j, d - 1], ring(d))

    def first(j):
        down(j).wait_recv()
        for d in (2, 1, 3):

            def put(a, n, v, d=d):
                ysend_l[j, d - 1, pl.ds(a, n), :] = v

            encode(l_blocks(lax.rem(y + d, 4), j), put)
            y_l(j, d).start()
        for k, b in enumerate(l_blocks(y, j)):
            own_l[j, k] = b

    goals = [(p, far), (sib, m), (sib, far), (at(-1), m), (at(-1), far)]

    def f_l(j, i):
        return send(fsend_l.at[j, i], frecv_l.at[j, i], fsl.at[j, i], frl.at[j, i], goals[i])

    def second(j):
        for d in (1, 2, 3):
            y_l(j, d).wait_recv()
        scales = [scale_of(yrecv_l.at[j, d], 384) for d in range(3)]
        for k in range(3):
            total = own_l[j, k]
            for d in range(3):
                total = total + decode(yrecv_l.at[j, d], k * LANES, LANES, scales[d])
            split[k, 0] = total[0:64]
            split[k, 1] = total[64:128]
        keep_l[j] = split[0, h]
        for i, (k, half) in enumerate([(0, 1 - h), (1, h), (1, 1 - h), (2, h), (2, 1 - h)]):

            def put(a, n, v, i=i):
                fsend_l[j, i, pl.ds(a, n), :] = v

            encode([split[k, half]], put)
            f_l(j, i).start()

    def third(j):
        for i in range(5):
            f_l(j, i).wait_recv()
        got = [decode(frecv_l.at[j, i], 0, 64, scale_of(frecv_l.at[j, i], 64)) for i in range(5)]
        finish(keep_l[j] + got[0], 2, j)
        finish(got[1] + got[2], 3 - 2 * core, j)
        finish(got[3] + got[4], 1 + 2 * core, j)

    first(0)
    first(1)
    second(0)
    first(2)
    second(1)
    third(0)
    first(3)
    second(2)
    third(1)
    second(3)
    third(2)
    third(3)

    beside.wait_send()

    @pl.when(core == 1)
    def _():
        up.wait_send()

    for note in notes:
        note.wait_send()
    f_e.wait_send()
    for d in (1, 2, 3):
        y_e(d).wait_send()
    for j in range(4):
        down(j).wait_send()
        for d in (1, 2, 3):
            y_l(j, d).wait_send()
        for i in range(5):
            f_l(j, i).wait_send()


def solution(mesh):
    parts, groups = mesh.shape["mesh"], mesh.shape["mem"]

    def per_device(x, coord, level):
        rows, width = x.shape
        owned = width // groups
        dma, vmem, i16 = pltpu.SemaphoreType.DMA, pltpu.VMEM, jnp.int16
        body = functools.partial(kernel, rows * groups, parts, 4.0 * width * parts, 12.0 * width)
        any_space, in_vmem = pl.BlockSpec(memory_space=pl.ANY), pl.BlockSpec(memory_space=pltpu.VMEM)
        return pl.pallas_call(
            body,
            out_shape=jax.ShapeDtypeStruct((owned, 4 * width), F32),
            in_specs=[any_space, in_vmem, in_vmem],
            out_specs=in_vmem,
            scratch_shapes=[
                vmem((4, rows, width), jnp.bfloat16),
                vmem((4, 3, LANES, rows), jnp.bfloat16),
                vmem((3, 1, width), jnp.int32),
                vmem((2, 2, 64, LANES), F32),
                vmem((4, 4, 64, LANES), F32),
                vmem((4, LANES, LANES), F32),
                vmem((4, 3, LANES, LANES), F32),
                vmem((4, 64, LANES), F32),
                vmem((4, 64, LANES), F32),
                vmem((3, 2, 64, LANES), F32),
                vmem((3, 528, LANES), i16),
                vmem((3, 528, LANES), i16),
                vmem((4, 3, 400, LANES), i16),
                vmem((4, 3, 400, LANES), i16),
                vmem((272, LANES), i16),
                vmem((272, LANES), i16),
                vmem((4, 5, 80, LANES), i16),
                vmem((4, 5, 80, LANES), i16),
                dma, dma((4,)), dma((4,)), dma, dma, dma, dma, dma((3,)), dma((3,)),
                dma((3,)), dma((3,)), dma((4, 3)), dma((4, 3)), dma, dma, dma((4, 5)), dma((4, 5)),
            ],
            compiler_params=pltpu.CompilerParams(
                collective_id=0, has_side_effects=True, vmem_limit_bytes=48 << 20
            ),
        )(x, coord.reshape(1, width), level.reshape(1, width))

    in_specs = (P("mem", "mesh"), P("mesh"), P("mesh"))
    out_specs = P(("mesh", "mem"), None)
    return jax.shard_map(per_device, mesh=mesh, in_specs=in_specs, out_specs=out_specs, check_vma=False)
```

```python
import functools

import jax
import jax.numpy as jnp
from jax import lax
from jax.experimental import pallas as pl
from jax.experimental.pallas import tpu as pltpu
from jax.sharding import PartitionSpec as P

MESH = pl.DeviceIdType.MESH
LANES = 128
STEPS = 32000.0
F32 = jnp.float32


def gc_taper(radius):
    r2 = radius * radius
    r3 = r2 * radius
    near = r3 * (0.625 + radius * (0.5 - 0.25 * radius)) - (5.0 / 3.0) * r2 + 1.0
    safe = jnp.maximum(radius, 1.0)
    s2 = safe * safe
    s3 = s2 * safe
    far = s3 * (0.625 + safe * (safe / 12.0 - 0.5)) + (5.0 / 3.0) * s2 - 5.0 * safe + 4.0 - 2.0 / (3.0 * safe)
    return jnp.where(radius <= 1.0, near, jnp.where(radius <= 2.0, far, 0.0))


def encode(blocks, store):
    top = functools.reduce(jnp.maximum, [jnp.max(jnp.abs(b), axis=0, keepdims=True) for b in blocks])
    power = jnp.ceil(jnp.log2(jnp.maximum(top, 1.2e-38)))
    half = jnp.floor(0.5 * power)
    one, two = jnp.exp2(-half), jnp.exp2(half - power) * STEPS
    at = 0
    for b in blocks:
        rows = b.shape[0]
        store(at, rows, jnp.round((b * one) * two).astype(jnp.int32).astype(jnp.int16))
        at += rows
    store(at, 16, jnp.broadcast_to(power, (16, LANES)).astype(jnp.int32).astype(jnp.int16))


def scale_of(ref, rows):
    power = ref[pl.ds(rows, 16), :].astype(jnp.int32).astype(F32)[0:1]
    half = jnp.floor(0.5 * power)
    return jnp.exp2(half), jnp.exp2(power - half) / STEPS


def decode(ref, at, rows, scale):
    return (ref[pl.ds(at, rows), :].astype(jnp.int32).astype(F32) * scale[0]) * scale[1]


def kernel(
    members, parts, period, reach,
    x_ref, coord_hbm, level_hbm, out_ref,
    coord_ref, level_ref, held, turned, coords, rowv, weight, own_e, own_l, keep_e, keep_l, split,
    ysend_e, yrecv_e, ysend_l, yrecv_l, fsend_e, frecv_e, fsend_l, frecv_l,
    own_sem, note_sem, zs, zr, bs, br, us, ur, cs, cr, yse, yre, ysl, yrl, fse, fre, fsl, frl,
):
    p, m = lax.axis_index("mesh"), lax.axis_index("mem")
    core, y, h = lax.rem(p, 2), m // 2, lax.rem(m, 2)
    far = m + 1 - 2 * h
    sib = p + 1 - 2 * core

    def at(shift):
        return lax.rem(p + shift + parts, parts)

    def ring(d):
        return (p, lax.rem(m + 2 * d, 8))

    mine = [
        pltpu.make_async_copy(x_ref, held.at[0], own_sem),
        pltpu.make_async_copy(coord_hbm, coord_ref, note_sem.at[0]),
        pltpu.make_async_copy(level_hbm, level_ref, note_sem.at[1]),
    ]
    for copy in mine:
        copy.start()

    barrier = pltpu.get_barrier_semaphore()
    peers = [(at(s), m) for s in (-3, -2, -1, 1, 2, 3)] + [ring(d) for d in (1, 2, 3)]
    peers += [(p, far), (at(1), far), (at(-1), far)]
    for peer in peers:
        pl.semaphore_signal(barrier, inc=1, device_id=peer, device_id_type=MESH)
    pl.semaphore_wait(barrier, len(peers))

    def send(src, dst, ssem, rsem, to):
        return pltpu.make_async_remote_copy(
            src_ref=src, dst_ref=dst, send_sem=ssem, recv_sem=rsem, device_id=to, device_id_type=MESH
        )

    piece, started = members // 32, [0, 0]

    def columns(j):
        return pl.ds(pl.multiple_of(j * LANES, LANES), LANES)

    def down(i):
        c, r = pl.ds(i // 4 * LANES, LANES), pl.ds(i % 4 * piece, piece)
        return send(x_ref.at[r, c], held.at[2, r, c], zs.at[i], zr.at[i], (at(-2), m))

    def pump(*counts):
        for who, count in enumerate(counts):
            if count:
                todo = range(started[who], started[who] + count)
                started[who] += count

                @pl.when(core == who)
                def _(todo=todo):
                    for i in todo:
                        if i >= 4:
                            down(i - 4).wait_send()
                        down(i).start()

    beside = send(x_ref, held.at[1], bs, br, (sib, m))
    up = send(x_ref, held.at[3], us, ur, (at(1), m))
    notes = [send(coord_hbm, coords.at[k], cs.at[k], cr.at[k], (at(-1 - k), m)) for k in range(3)]
    for note in notes:
        note.start()
    beside.start()

    @pl.when(core == 1)
    def _():
        up.start()

    pump(4, 0)
    for copy in mine:
        copy.wait()

    def turn(slot, to):
        def body(q, carry):
            turned[q, to] = held[slot, :, columns(q)].T
            return carry

        lax.fori_loop(0, 4, body, 0)

    turn(0, 0)

    def e_blocks(row):
        full = jnp.dot(turned[row, 0], held[0], preferred_element_type=F32)
        return [full[:, k * LANES : (k + 1) * LANES] for k in range(4)]

    def y_e(d):
        return send(ysend_e.at[d - 1], yrecv_e.at[d - 1], yse.at[d - 1], yre.at[d - 1], ring(d))

    for d in (2, 1, 3):

        def put(a, n, v, d=d):
            ysend_e[d - 1, pl.ds(a, n), :] = v

        encode(e_blocks(lax.rem(y + d, 4)), put)
        y_e(d).start()
    for k, b in enumerate(e_blocks(y)):
        own_e[k] = b

    pump(3, 3)

    def as_rows(ref):
        line = ref[0:1, columns(y)].astype(F32)
        return jnp.broadcast_to(line, (LANES, LANES)).T

    for k, ref in enumerate((coord_ref, level_ref)):
        v = as_rows(ref)
        rowv[k, 0] = v[0:64]
        rowv[k, 1] = v[64:128]
    row = rowv[0, h]
    limit = 0.05 * rowv[1, h]
    for note in notes:
        note.wait_recv()
    for s in range(4):
        for j in range(4):
            c = pl.ds(j * LANES, LANES)
            col = (coord_ref[0:1, c] if s == 0 else coords[s - 1, 0:1, c]).astype(F32)
            gap = col - row
            gap = jnp.where(gap < 0.0, gap + period, gap)
            dist = jnp.minimum(gap, period - gap)
            weight[s, j] = gc_taper(dist / reach) * (1.0 / (members - 1.0))

    def finish(value, s, j):
        c = weight[s, j] * value
        out_ref[:, pl.ds(pl.multiple_of((s * 4 + j) * LANES, LANES), LANES)] = c - jnp.clip(c, -limit, limit)

    beside.wait_recv()
    turn(1, 1)
    pump(3, 3)

    f_e = send(fsend_e, frecv_e, fse, fre, (p, far))
    for d in (1, 2, 3):
        y_e(d).wait_recv()
    scales = [scale_of(yrecv_e.at[d], 512) for d in range(3)]
    theirs = []
    for k in range(4):
        total = own_e[k]
        for d in range(3):
            total = total + decode(yrecv_e.at[d], k * LANES, LANES, scales[d])
        split[0, 0] = total[0:64]
        split[0, 1] = total[64:128]
        keep_e[k] = split[0, h]
        theirs.append(split[0, 1 - h])

    def put_e(a, n, v):
        fsend_e[pl.ds(a, n), :] = v

    encode(theirs, put_e)
    f_e.start()
    for _ in range(4):
        pump(1, 1)

    @pl.when(core == 0)
    def _():
        up.wait_recv()
        turn(3, 2)

    def third_e():
        f_e.wait_recv()
        scale = scale_of(frecv_e, 256)
        for k in range(4):
            finish(keep_e[k] + decode(frecv_e, k * 64, 64, scale), 0, k)

    lhs2, rhs2 = 1 + (1 - core), 2 * (1 - core)

    def l_blocks(row, j):
        c = pl.ds(j * LANES, LANES)
        pair = turned[row, 0:2].reshape(2 * LANES, members // 8)
        both = jnp.dot(pair, held[2, :, c], preferred_element_type=F32)
        third = jnp.dot(turned[row, lhs2], held[rhs2, :, c], preferred_element_type=F32)
        return [both[0:LANES], both[LANES:], third]

    def y_l(j, d):
        return send(ysend_l.at[j, d - 1], yrecv_l.at[j, d - 1], ysl.at[j, d - 1], yrl.at[j, d - 1], ring(d))

    def first(j):
        for i in range(4):
            down(4 * j + i).wait_recv()
        for d in (2, 1, 3):

            def put(a, n, v, d=d):
                ysend_l[j, d - 1, pl.ds(a, n), :] = v

            encode(l_blocks(lax.rem(y + d, 4), j), put)
            y_l(j, d).start()
        for k, b in enumerate(l_blocks(y, j)):
            own_l[j, k] = b

    goals = [(p, far), (sib, m), (sib, far), (at(-1), m), (at(-1), far)]

    def f_l(j, i):
        return send(fsend_l.at[j, i], frecv_l.at[j, i], fsl.at[j, i], frl.at[j, i], goals[i])

    def second(j):
        for d in (1, 2, 3):
            y_l(j, d).wait_recv()
        scales = [scale_of(yrecv_l.at[j, d], 384) for d in range(3)]
        for k in range(3):
            total = own_l[j, k]
            for d in range(3):
                total = total + decode(yrecv_l.at[j, d], k * LANES, LANES, scales[d])
            split[k, 0] = total[0:64]
            split[k, 1] = total[64:128]
        keep_l[j] = split[0, h]
        for i, (k, half) in enumerate([(0, 1 - h), (1, h), (1, 1 - h), (2, h), (2, 1 - h)]):

            def put(a, n, v, i=i):
                fsend_l[j, i, pl.ds(a, n), :] = v

            encode([split[k, half]], put)
            f_l(j, i).start()

    def third(j):
        for i in range(5):
            f_l(j, i).wait_recv()
        got = [decode(frecv_l.at[j, i], 0, 64, scale_of(frecv_l.at[j, i], 64)) for i in range(5)]
        finish(keep_l[j] + got[0], 2, j)
        finish(got[1] + got[2], 3 - 2 * core, j)
        finish(got[3] + got[4], 1 + 2 * core, j)

    first(0)
    pump(1, 1)
    first(1)
    pump(1, 1)
    second(0)
    pump(0, 2)
    pump(0, 2)
    first(2)
    second(1)
    first(3)
    third_e()
    third(0)
    second(2)
    third(1)
    second(3)
    third(2)
    third(3)
    assert started == [16, 16]

    beside.wait_send()

    @pl.when(core == 1)
    def _():
        up.wait_send()

    for note in notes:
        note.wait_send()
    f_e.wait_send()
    for d in (1, 2, 3):
        y_e(d).wait_send()
    for i in range(12, 16):
        down(i).wait_send()
    for j in range(4):
        for d in (1, 2, 3):
            y_l(j, d).wait_send()
        for i in range(5):
            f_l(j, i).wait_send()


def solution(mesh):
    parts, groups = mesh.shape["mesh"], mesh.shape["mem"]

    def per_device(x, coord, level):
        rows, width = x.shape
        owned = width // groups
        dma, vmem, i16 = pltpu.SemaphoreType.DMA, pltpu.VMEM, jnp.int16
        body = functools.partial(kernel, rows * groups, parts, 4.0 * width * parts, 12.0 * width)
        in_hbm = pl.BlockSpec(memory_space=pltpu.HBM)
        return pl.pallas_call(
            body,
            out_shape=jax.ShapeDtypeStruct((owned, 4 * width), F32),
            in_specs=[in_hbm] * 3,
            out_specs=pl.BlockSpec(memory_space=pltpu.VMEM),
            scratch_shapes=[
                vmem((1, width), jnp.int32),
                vmem((1, width), jnp.int32),
                vmem((4, rows, width), jnp.bfloat16),
                vmem((4, 3, LANES, rows), jnp.bfloat16),
                vmem((3, 1, width), jnp.int32),
                vmem((2, 2, 64, LANES), F32),
                vmem((4, 4, 64, LANES), F32),
                vmem((4, LANES, LANES), F32),
                vmem((4, 3, LANES, LANES), F32),
                vmem((4, 64, LANES), F32),
                vmem((4, 64, LANES), F32),
                vmem((3, 2, 64, LANES), F32),
                vmem((3, 528, LANES), i16),
                vmem((3, 528, LANES), i16),
                vmem((4, 3, 400, LANES), i16),
                vmem((4, 3, 400, LANES), i16),
                vmem((272, LANES), i16),
                vmem((272, LANES), i16),
                vmem((4, 5, 80, LANES), i16),
                vmem((4, 5, 80, LANES), i16),
                dma, dma((2,)), dma((16,)), dma((16,)), dma, dma, dma, dma, dma((3,)), dma((3,)),
                dma((3,)), dma((3,)), dma((4, 3)), dma((4, 3)), dma, dma, dma((4, 5)), dma((4, 5)),
            ],
            compiler_params=pltpu.CompilerParams(
                collective_id=0, has_side_effects=True, vmem_limit_bytes=67043328
            ),
        )(x, coord.reshape(1, width), level.reshape(1, width))

    in_specs = (P("mem", "mesh"), P("mesh"), P("mesh"))
    out_specs = P(("mesh", "mem"), None)
    return jax.shard_map(per_device, mesh=mesh, in_specs=in_specs, out_specs=out_specs, check_vma=False)
```

```python
import functools

import jax
import jax.numpy as jnp
from jax import lax
from jax.experimental import pallas as pl
from jax.experimental.pallas import tpu as pltpu
from jax.sharding import PartitionSpec as P

MESH = pl.DeviceIdType.MESH
LANES = 128
STEPS = 32000.0
F32 = jnp.float32


def gc_taper(radius):
    r2 = radius * radius
    r3 = r2 * radius
    near = r3 * (0.625 + radius * (0.5 - 0.25 * radius)) - (5.0 / 3.0) * r2 + 1.0
    safe = jnp.maximum(radius, 1.0)
    s2 = safe * safe
    s3 = s2 * safe
    far = s3 * (0.625 + safe * (safe / 12.0 - 0.5)) + (5.0 / 3.0) * s2 - 5.0 * safe + 4.0 - 2.0 / (3.0 * safe)
    return jnp.where(radius <= 1.0, near, jnp.where(radius <= 2.0, far, 0.0))


def encode(blocks, store):
    top = functools.reduce(jnp.maximum, [jnp.max(jnp.abs(b), axis=0, keepdims=True) for b in blocks])
    power = jnp.ceil(jnp.log2(jnp.maximum(top, 1.2e-38)))
    half = jnp.floor(0.5 * power)
    one, two = jnp.exp2(-half), jnp.exp2(half - power) * STEPS
    at = 0
    for b in blocks:
        rows = b.shape[0]
        store(at, rows, jnp.round((b * one) * two).astype(jnp.int32).astype(jnp.int16))
        at += rows
    store(at, 16, jnp.broadcast_to(power, (16, LANES)).astype(jnp.int32).astype(jnp.int16))


def scale_of(ref, rows):
    power = ref[pl.ds(rows, 16), :].astype(jnp.int32).astype(F32)[0:1]
    half = jnp.floor(0.5 * power)
    return jnp.exp2(half), jnp.exp2(power - half) / STEPS


def decode(ref, at, rows, scale):
    return (ref[pl.ds(at, rows), :].astype(jnp.int32).astype(F32) * scale[0]) * scale[1]


def kernel(
    members, parts, period, reach,
    x_ref, coord_hbm, level_hbm, out_ref,
    coord_ref, level_ref, held, turned, coords, rowv, weight, own_e, own_l, keep_e, keep_l, split,
    ysend_e, yrecv_e, ysend_m, yrecv_m, ysend_s, yrecv_s, fsend_e, frecv_e, fsend_l, frecv_l,
    own_sem, note_sem, zs, zr, bs, br, us, ur, cs, cr, yse, yre, ysm, yrm, yss, yrs, fse, fre, fsl, frl,
):
    p, m = lax.axis_index("mesh"), lax.axis_index("mem")
    core, y, h = lax.rem(p, 2), m // 2, lax.rem(m, 2)
    far = m + 1 - 2 * h
    sib = p + 1 - 2 * core

    def at(shift):
        return lax.rem(p + shift + parts, parts)

    def ring(d):
        return (p, lax.rem(m + 2 * d, 8))

    mine = [
        pltpu.make_async_copy(x_ref, held.at[0], own_sem),
        pltpu.make_async_copy(coord_hbm, coord_ref, note_sem.at[0]),
        pltpu.make_async_copy(level_hbm, level_ref, note_sem.at[1]),
    ]
    for copy in mine:
        copy.start()

    barrier = pltpu.get_barrier_semaphore()
    peers = [(at(s), m) for s in (-3, -2, -1, 1, 2, 3)] + [ring(d) for d in (1, 2, 3)]
    peers += [(p, far), (at(1), far), (at(-1), far)]
    for peer in peers:
        pl.semaphore_signal(barrier, inc=1, device_id=peer, device_id_type=MESH)
    pl.semaphore_wait(barrier, len(peers))

    def send(src, dst, ssem, rsem, to):
        return pltpu.make_async_remote_copy(
            src_ref=src, dst_ref=dst, send_sem=ssem, recv_sem=rsem, device_id=to, device_id_type=MESH
        )

    piece, started = members // 32, [0, 0]

    def columns(j):
        return pl.ds(pl.multiple_of(j * LANES, LANES), LANES)

    def down(i):
        c, r = pl.ds(i // 4 * LANES, LANES), pl.ds(i % 4 * piece, piece)
        return send(x_ref.at[r, c], held.at[2, r, c], zs.at[i], zr.at[i], (at(-2), m))

    def pump(who, count):
        for i in range(started[who], started[who] + count):
            if i >= 4:
                down(i - 4).wait_send()
            down(i).start()
        started[who] += count

    beside = send(x_ref, held.at[1], bs, br, (sib, m))
    up = send(x_ref, held.at[3], us, ur, (at(1), m))
    notes = [send(coord_hbm, coords.at[k], cs.at[k], cr.at[k], (at(-1 - k), m)) for k in range(3)]
    for note in notes:
        note.start()
    beside.start()

    @pl.when(core == 0)
    def _():
        pump(0, 4)

    @pl.when(core == 1)
    def _():
        up.start()

    for copy in mine:
        copy.wait()

    def turn(slot, to):
        def body(q, carry):
            turned[q, to] = held[slot, :, columns(q)].T
            return carry

        lax.fori_loop(0, 4, body, 0)

    turn(0, 0)

    def e_blocks(row):
        full = jnp.dot(turned[row, 0], held[0], preferred_element_type=F32)
        return [full[:, k * LANES : (k + 1) * LANES] for k in range(4)]

    def y_e(d):
        return send(ysend_e.at[d - 1], yrecv_e.at[d - 1], yse.at[d - 1], yre.at[d - 1], ring(d))

    for d in (2, 1, 3):

        def put(a, n, v, d=d):
            ysend_e[d - 1, pl.ds(a, n), :] = v

        encode(e_blocks(lax.rem(y + d, 4)), put)
        y_e(d).start()
    for k, b in enumerate(e_blocks(y)):
        own_e[k] = b

    @pl.when(core == 0)
    def _():
        pump(0, 3)

    @pl.when(core == 1)
    def _():
        pump(1, 3)

    def as_rows(ref):
        line = ref[0:1, columns(y)].astype(F32)
        return jnp.broadcast_to(line, (LANES, LANES)).T

    for k, ref in enumerate((coord_ref, level_ref)):
        v = as_rows(ref)
        rowv[k, 0] = v[0:64]
        rowv[k, 1] = v[64:128]
    row = rowv[0, h]
    limit = 0.05 * rowv[1, h]
    for note in notes:
        note.wait_recv()
    for s in range(4):
        for j in range(4):
            c = pl.ds(j * LANES, LANES)
            col = (coord_ref[0:1, c] if s == 0 else coords[s - 1, 0:1, c]).astype(F32)
            gap = col - row
            gap = jnp.where(gap < 0.0, gap + period, gap)
            dist = jnp.minimum(gap, period - gap)
            weight[s, j] = gc_taper(dist / reach) * (1.0 / (members - 1.0))

    def finish(value, s, j):
        c = weight[s, j] * value
        out_ref[:, pl.ds(pl.multiple_of((s * 4 + j) * LANES, LANES), LANES)] = c - jnp.clip(c, -limit, limit)

    beside.wait_recv()
    turn(1, 1)
    deep = parts // 4
    z = lax.rem(p // 2, deep)
    ends = jnp.logical_or(z == 0, z == deep - 1)
    waiting = {0: [], 1: []}

    def launch(who, *copies):
        if waiting[who] is None:
            for copy in copies:
                copy.start()
        else:
            waiting[who] += copies

            @pl.when(jnp.logical_not(ends))
            def _():
                for copy in copies:
                    copy.start()

    def flush(who):
        @pl.when(ends)
        def _():
            for copy in waiting[who]:
                copy.start()

        waiting[who] = None

    f_e = send(fsend_e, frecv_e, fse, fre, (p, far))

    def e_second(who):
        for d in (1, 2, 3):
            y_e(d).wait_recv()
        scales = [scale_of(yrecv_e.at[d], 512) for d in range(3)]
        theirs = []
        for k in range(4):
            total = own_e[k]
            for d in range(3):
                total = total + decode(yrecv_e.at[d], k * LANES, LANES, scales[d])
            split[0, 0] = total[0:64]
            split[0, 1] = total[64:128]
            keep_e[k] = split[0, h]
            theirs.append(split[0, 1 - h])

        def put(a, n, v):
            fsend_e[pl.ds(a, n), :] = v

        encode(theirs, put)
        launch(who, f_e)

    def e_third():
        f_e.wait_recv()
        scale = scale_of(frecv_e, 256)
        for k in range(4):
            finish(keep_e[k] + decode(frecv_e, k * 64, 64, scale), 0, k)

    def y_m(j, d):
        return send(ysend_m.at[j, d - 1], yrecv_m.at[j, d - 1], ysm.at[j, d - 1], yrm.at[j, d - 1], ring(d))

    def y_s(j, d):
        return send(ysend_s.at[j, d - 1], yrecv_s.at[j, d - 1], yss.at[j, d - 1], yrs.at[j, d - 1], ring(d))

    def m_blocks(row, j):
        pair = turned[row, 0:2].reshape(2 * LANES, members // 8)
        both = jnp.dot(pair, held[2, :, pl.ds(j * LANES, LANES)], preferred_element_type=F32)
        return [both[0:LANES], both[LANES:]]

    def m_first(j):
        for i in range(4):
            down(4 * j + i).wait_recv()
        for d in (2, 1, 3):

            def put(a, n, v, d=d):
                ysend_m[j, d - 1, pl.ds(a, n), :] = v

            encode(m_blocks(lax.rem(y + d, 4), j), put)
            y_m(j, d).start()
        for k, b in enumerate(m_blocks(y, j)):
            own_l[j, k] = b

    def s_first(j, left, right):
        rhs = held.at[right, :, pl.ds(j * LANES, LANES)]
        for d in (2, 1, 3):

            def put(a, n, v, d=d):
                ysend_s[j, d - 1, pl.ds(a, n), :] = v

            encode([jnp.dot(turned[lax.rem(y + d, 4), left], rhs[...], preferred_element_type=F32)], put)
            y_s(j, d).start()
        own_l[j, 2] = jnp.dot(turned[y, left], rhs[...], preferred_element_type=F32)

    goals = [(p, far), (sib, m), (sib, far), (at(-1), m), (at(-1), far)]

    def f_l(j, i):
        return send(fsend_l.at[j, i], frecv_l.at[j, i], fsl.at[j, i], frl.at[j, i], goals[i])

    def gathered(j, k, recv, at_row, scales):
        total = own_l[j, k]
        for d in range(3):
            total = total + decode(recv.at[j, d], at_row, LANES, scales[d])
        split[k, 0] = total[0:64]
        split[k, 1] = total[64:128]

    def forward(who, j, i, value):
        def put(a, n, v):
            fsend_l[j, i, pl.ds(a, n), :] = v

        encode([value], put)
        if i == 1:
            f_l(j, i).start()
        else:
            launch(who, f_l(j, i))

    def m_second(who, j):
        for d in (1, 2, 3):
            y_m(j, d).wait_recv()
        scales = [scale_of(yrecv_m.at[j, d], 256) for d in range(3)]
        gathered(j, 0, yrecv_m, 0, scales)
        forward(who, j, 0, split[0, 1 - h])
        gathered(j, 1, yrecv_m, LANES, scales)
        forward(who, j, 2, split[1, 1 - h])
        forward(who, j, 1, split[1, h])
        keep_l[j] = split[0, h]

    def s_second(who, j):
        for d in (1, 2, 3):
            y_s(j, d).wait_recv()
        gathered(j, 2, yrecv_s, 0, [scale_of(yrecv_s.at[j, d], 128) for d in range(3)])
        forward(who, j, 4, split[2, 1 - h])
        forward(who, j, 3, split[2, h])

    def got(j, i):
        f_l(j, i).wait_recv()
        return decode(frecv_l.at[j, i], 0, 64, scale_of(frecv_l.at[j, i], 64))

    def third_a(j):
        finish(keep_l[j] + got(j, 0), 2, j)

    def third_b(j):
        finish(got(j, 1) + got(j, 2), 3 - 2 * core, j)

    def third_c(j):
        finish(got(j, 3) + got(j, 4), 1 + 2 * core, j)

    @pl.when(core == 0)
    def _():
        pump(0, 1)
        m_first(0)
        pump(0, 2)
        e_second(0)
        pump(0, 1)
        m_first(1)
        pump(0, 2)
        m_second(0, 0)
        pump(0, 1)
        up.wait_recv()
        turn(3, 2)
        pump(0, 1)
        s_first(0, 2, 2)
        s_first(1, 2, 2)
        pump(0, 1)
        m_first(2)
        m_second(0, 1)
        s_first(2, 2, 2)
        s_second(0, 0)
        s_second(0, 1)
        m_first(3)
        s_first(3, 2, 2)
        m_second(0, 2)
        s_second(0, 2)
        flush(0)
        s_second(0, 3)
        m_second(0, 3)

    @pl.when(core == 1)
    def _():
        pump(1, 1)
        s_first(0, 1, 0)
        s_first(1, 1, 0)
        pump(1, 2)
        s_first(2, 1, 0)
        s_first(3, 1, 0)
        pump(1, 2)
        e_second(1)
        m_first(0)
        pump(1, 1)
        s_second(1, 0)
        s_second(1, 1)
        pump(1, 1)
        s_second(1, 2)
        s_second(1, 3)
        pump(1, 2)
        m_first(1)
        pump(1, 1)
        m_second(1, 0)
        pump(1, 3)
        m_first(2)
        m_second(1, 1)
        m_second(1, 2)
        m_first(3)
        flush(1)
        m_second(1, 3)

    e_third()
    for j in range(4):
        third_c(j)
        third_a(j)
        third_b(j)
    assert started == [16, 16]

    beside.wait_send()

    @pl.when(core == 1)
    def _():
        up.wait_send()

    for note in notes:
        note.wait_send()
    f_e.wait_send()
    for d in (1, 2, 3):
        y_e(d).wait_send()
    for i in range(12, 16):
        down(i).wait_send()
    for j in range(4):
        for d in (1, 2, 3):
            y_m(j, d).wait_send()
            y_s(j, d).wait_send()
        for i in range(5):
            f_l(j, i).wait_send()


def solution(mesh):
    parts, groups = mesh.shape["mesh"], mesh.shape["mem"]

    def per_device(x, coord, level):
        rows, width = x.shape
        owned = width // groups
        dma, vmem, i16 = pltpu.SemaphoreType.DMA, pltpu.VMEM, jnp.int16
        body = functools.partial(kernel, rows * groups, parts, 4.0 * width * parts, 12.0 * width)
        in_hbm = pl.BlockSpec(memory_space=pltpu.HBM)
        return pl.pallas_call(
            body,
            out_shape=jax.ShapeDtypeStruct((owned, 4 * width), F32),
            in_specs=[in_hbm] * 3,
            out_specs=pl.BlockSpec(memory_space=pltpu.VMEM),
            scratch_shapes=[
                vmem((1, width), jnp.int32),
                vmem((1, width), jnp.int32),
                vmem((4, rows, width), jnp.bfloat16),
                vmem((4, 3, LANES, rows), jnp.bfloat16),
                vmem((3, 1, width), jnp.int32),
                vmem((2, 2, 64, LANES), F32),
                vmem((4, 4, 64, LANES), F32),
                vmem((4, LANES, LANES), F32),
                vmem((4, 3, LANES, LANES), F32),
                vmem((4, 64, LANES), F32),
                vmem((4, 64, LANES), F32),
                vmem((3, 2, 64, LANES), F32),
                vmem((3, 528, LANES), i16),
                vmem((3, 528, LANES), i16),
                vmem((4, 3, 272, LANES), i16),
                vmem((4, 3, 272, LANES), i16),
                vmem((4, 3, 144, LANES), i16),
                vmem((4, 3, 144, LANES), i16),
                vmem((272, LANES), i16),
                vmem((272, LANES), i16),
                vmem((4, 5, 80, LANES), i16),
                vmem((4, 5, 80, LANES), i16),
                dma, dma((2,)), dma((16,)), dma((16,)), dma, dma, dma, dma, dma((3,)), dma((3,)),
                dma((3,)), dma((3,)), dma((4, 3)), dma((4, 3)), dma((4, 3)), dma((4, 3)), dma, dma, dma((4, 5)), dma((4, 5)),
            ],
            compiler_params=pltpu.CompilerParams(
                collective_id=0, has_side_effects=True, vmem_limit_bytes=67043328
            ),
        )(x, coord.reshape(1, width), level.reshape(1, width))

    in_specs = (P("mem", "mesh"), P("mesh"), P("mesh"))
    out_specs = P(("mesh", "mem"), None)
    return jax.shard_map(per_device, mesh=mesh, in_specs=in_specs, out_specs=out_specs, check_vma=False)
```

```python
import functools

import jax
import jax.numpy as jnp
from jax import lax
from jax.experimental import pallas as pl
from jax.experimental.pallas import tpu as pltpu
from jax.sharding import PartitionSpec as P

MESH = pl.DeviceIdType.MESH
LANES = 128
STEPS = 32000.0
F32 = jnp.float32


def gc_taper(radius):
    r2 = radius * radius
    r3 = r2 * radius
    near = r3 * (0.625 + radius * (0.5 - 0.25 * radius)) - (5.0 / 3.0) * r2 + 1.0
    safe = jnp.maximum(radius, 1.0)
    s2 = safe * safe
    s3 = s2 * safe
    far = s3 * (0.625 + safe * (safe / 12.0 - 0.5)) + (5.0 / 3.0) * s2 - 5.0 * safe + 4.0 - 2.0 / (3.0 * safe)
    return jnp.where(radius <= 1.0, near, jnp.where(radius <= 2.0, far, 0.0))


def encode(blocks, store):
    top = functools.reduce(jnp.maximum, [jnp.max(jnp.abs(b), axis=0, keepdims=True) for b in blocks])
    power = jnp.ceil(jnp.log2(jnp.maximum(top, 1.2e-38)))
    half = jnp.floor(0.5 * power)
    one, two = jnp.exp2(-half), jnp.exp2(half - power) * STEPS
    at = 0
    for b in blocks:
        rows = b.shape[0]
        store(at, rows, jnp.round((b * one) * two).astype(jnp.int32).astype(jnp.int16))
        at += rows
    store(at, 16, jnp.broadcast_to(power, (16, LANES)).astype(jnp.int32).astype(jnp.int16))


def scale_of(ref, rows):
    power = ref[pl.ds(rows, 16), :].astype(jnp.int32).astype(F32)[0:1]
    half = jnp.floor(0.5 * power)
    return jnp.exp2(half), jnp.exp2(power - half) / STEPS


def decode(ref, at, rows, scale):
    return (ref[pl.ds(at, rows), :].astype(jnp.int32).astype(F32) * scale[0]) * scale[1]


def kernel(
    members, parts, period, reach,
    x_ref, coord_hbm, level_hbm, out_ref,
    coord_ref, level_ref, held, turned, begun, coords, rowv, weight, own_e, own_l, keep_e, keep_l, split,
    ysend_e, yrecv_e, ysend_m, yrecv_m, ysend_s, yrecv_s, fsend_e, frecv_e, fsend_l, frecv_l,
    own_sem, note_sem, zs, zr, bs, br, us, ur, cs, cr, yse, yre, ysm, yrm, yss, yrs, fse, fre, fsl, frl,
):
    p, m = lax.axis_index("mesh"), lax.axis_index("mem")
    core, y, h = lax.rem(p, 2), m // 2, lax.rem(m, 2)
    far = m + 1 - 2 * h
    sib = p + 1 - 2 * core

    def at(shift):
        return lax.rem(p + shift + parts, parts)

    def ring(d):
        return (p, lax.rem(m + 2 * d, 8))

    mine = [
        pltpu.make_async_copy(x_ref, held.at[0], own_sem),
        pltpu.make_async_copy(coord_hbm, coord_ref, note_sem.at[0]),
        pltpu.make_async_copy(level_hbm, level_ref, note_sem.at[1]),
    ]
    for copy in mine:
        copy.start()

    barrier = pltpu.get_barrier_semaphore()
    peers = [(at(s), m) for s in (-3, -2, -1, 1, 2, 3)] + [ring(d) for d in (1, 2, 3)]
    peers += [(p, far), (at(1), far), (at(-1), far)]
    for peer in peers:
        pl.semaphore_signal(barrier, inc=1, device_id=peer, device_id_type=MESH)
    pl.semaphore_wait(barrier, len(peers))

    def send(src, dst, ssem, rsem, to):
        return pltpu.make_async_remote_copy(
            src_ref=src, dst_ref=dst, send_sem=ssem, recv_sem=rsem, device_id=to, device_id_type=MESH
        )

    piece, started = members // 32, [0, 0]

    def columns(j):
        return pl.ds(pl.multiple_of(j * LANES, LANES), LANES)

    def down(i):
        c, r = pl.ds(i // 4 * LANES, LANES), pl.ds(i % 4 * piece, piece)
        return send(x_ref.at[r, c], held.at[2, r, c], zs.at[i], zr.at[i], (at(-2), m))

    def pump(who, count):
        for i in range(started[who], started[who] + count):
            if i >= 4:
                down(i - 4).wait_send()
            down(i).start()
        started[who] += count

    beside = send(x_ref, held.at[1], bs, br, (sib, m))
    up = send(x_ref, held.at[3], us, ur, (at(1), m))
    notes = [send(coord_hbm, coords.at[k], cs.at[k], cr.at[k], (at(-1 - k), m)) for k in range(3)]
    for note in notes:
        note.start()
    beside.start()

    @pl.when(core == 0)
    def _():
        pump(0, 4)

    @pl.when(core == 1)
    def _():
        up.start()

    for copy in mine:
        copy.wait()

    def turn(slot, to):
        def body(q, carry):
            turned[q, to] = held[slot, :, columns(q)].T
            return carry

        lax.fori_loop(0, 4, body, 0)

    turn(0, 0)

    def e_blocks(row):
        full = jnp.dot(turned[row, 0], held[0], preferred_element_type=F32)
        return [full[:, k * LANES : (k + 1) * LANES] for k in range(4)]

    def y_e(d):
        return send(ysend_e.at[d - 1], yrecv_e.at[d - 1], yse.at[d - 1], yre.at[d - 1], ring(d))

    for d in (2, 1, 3):

        def put(a, n, v, d=d):
            ysend_e[d - 1, pl.ds(a, n), :] = v

        encode(e_blocks(lax.rem(y + d, 4)), put)
        y_e(d).start()
    for k, b in enumerate(e_blocks(y)):
        own_e[k] = b

    @pl.when(core == 0)
    def _():
        pump(0, 3)

    @pl.when(core == 1)
    def _():
        pump(1, 3)

    def as_rows(ref):
        line = ref[0:1, columns(y)].astype(F32)
        return jnp.broadcast_to(line, (LANES, LANES)).T

    for k, ref in enumerate((coord_ref, level_ref)):
        v = as_rows(ref)
        rowv[k, 0] = v[0:64]
        rowv[k, 1] = v[64:128]
    row = rowv[0, h]
    limit = 0.05 * rowv[1, h]
    for note in notes:
        note.wait_recv()
    for s in range(4):
        for j in range(4):
            c = pl.ds(j * LANES, LANES)
            col = (coord_ref[0:1, c] if s == 0 else coords[s - 1, 0:1, c]).astype(F32)
            gap = col - row
            gap = jnp.where(gap < 0.0, gap + period, gap)
            dist = jnp.minimum(gap, period - gap)
            weight[s, j] = gc_taper(dist / reach) * (1.0 / (members - 1.0))

    def finish(value, s, j):
        c = weight[s, j] * value
        out_ref[:, pl.ds(pl.multiple_of((s * 4 + j) * LANES, LANES), LANES)] = c - jnp.clip(c, -limit, limit)

    beside.wait_recv()
    turn(1, 1)
    f_e = send(fsend_e, frecv_e, fse, fre, (p, far))

    def e_second():
        for d in (1, 2, 3):
            y_e(d).wait_recv()
        scales = [scale_of(yrecv_e.at[d], 512) for d in range(3)]
        theirs = []
        for k in range(4):
            total = own_e[k]
            for d in range(3):
                total = total + decode(yrecv_e.at[d], k * LANES, LANES, scales[d])
            split[0, 0] = total[0:64]
            split[0, 1] = total[64:128]
            keep_e[k] = split[0, h]
            theirs.append(split[0, 1 - h])

        def put(a, n, v):
            fsend_e[pl.ds(a, n), :] = v

        encode(theirs, put)
        f_e.start()

    def e_third():
        f_e.wait_recv()
        scale = scale_of(frecv_e, 256)
        for k in range(4):
            finish(keep_e[k] + decode(frecv_e, k * 64, 64, scale), 0, k)

    def y_m(j, d):
        return send(ysend_m.at[j, d - 1], yrecv_m.at[j, d - 1], ysm.at[j, d - 1], yrm.at[j, d - 1], ring(d))

    def y_s(j, d):
        return send(ysend_s.at[j, d - 1], yrecv_s.at[j, d - 1], yss.at[j, d - 1], yrs.at[j, d - 1], ring(d))

    depth = members // 8
    head = depth * 2 // 3

    def m_product(row, j, start, size):
        k = pl.ds(start, size)
        pair = turned[row, 0:2, :, k].reshape(2 * LANES, size)
        return jnp.dot(pair, held[2, k, pl.ds(j * LANES, LANES)], preferred_element_type=F32)

    def m_blocks(d, j):
        row = lax.rem(y + d, 4)
        if j < 3:
            both = m_product(row, j, 0, depth)
        else:
            both = begun[d] + m_product(row, j, head, depth - head)
        return [both[0:LANES], both[LANES:]]

    def m_first(j):
        for i in range(3):
            down(4 * j + i).wait_recv()
        if j == 3:
            for d in range(4):
                begun[d] = m_product(lax.rem(y + d, 4), j, 0, head)
        down(4 * j + 3).wait_recv()
        for d in (2, 1, 3):

            def put(a, n, v, d=d):
                ysend_m[j, d - 1, pl.ds(a, n), :] = v

            encode(m_blocks(d, j), put)
            y_m(j, d).start()
        for k, b in enumerate(m_blocks(0, j)):
            own_l[j, k] = b

    def s_first(j, left, right):
        rhs = held.at[right, :, pl.ds(j * LANES, LANES)]
        for d in (2, 1, 3):

            def put(a, n, v, d=d):
                ysend_s[j, d - 1, pl.ds(a, n), :] = v

            encode([jnp.dot(turned[lax.rem(y + d, 4), left], rhs[...], preferred_element_type=F32)], put)
            y_s(j, d).start()
        own_l[j, 2] = jnp.dot(turned[y, left], rhs[...], preferred_element_type=F32)

    goals = [(p, far), (sib, m), (sib, far), (at(-1), m), (at(-1), far)]

    def f_l(j, i):
        return send(fsend_l.at[j, i], frecv_l.at[j, i], fsl.at[j, i], frl.at[j, i], goals[i])

    def gathered(j, k, recv, at_row, scales):
        total = own_l[j, k]
        for d in range(3):
            total = total + decode(recv.at[j, d], at_row, LANES, scales[d])
        split[k, 0] = total[0:64]
        split[k, 1] = total[64:128]

    def forward(j, i, value):
        def put(a, n, v):
            fsend_l[j, i, pl.ds(a, n), :] = v

        encode([value], put)
        f_l(j, i).start()

    def m_second(j):
        for d in (1, 2, 3):
            y_m(j, d).wait_recv()
        scales = [scale_of(yrecv_m.at[j, d], 256) for d in range(3)]
        gathered(j, 0, yrecv_m, 0, scales)
        forward(j, 0, split[0, 1 - h])
        gathered(j, 1, yrecv_m, LANES, scales)
        forward(j, 2, split[1, 1 - h])
        forward(j, 1, split[1, h])
        keep_l[j] = split[0, h]

    def s_second(j):
        for d in (1, 2, 3):
            y_s(j, d).wait_recv()
        gathered(j, 2, yrecv_s, 0, [scale_of(yrecv_s.at[j, d], 128) for d in range(3)])
        forward(j, 4, split[2, 1 - h])
        forward(j, 3, split[2, h])

    def got(j, i):
        f_l(j, i).wait_recv()
        return decode(frecv_l.at[j, i], 0, 64, scale_of(frecv_l.at[j, i], 64))

    def third_a(j):
        finish(keep_l[j] + got(j, 0), 2, j)

    def third_b(j):
        finish(got(j, 1) + got(j, 2), 3 - 2 * core, j)

    def third_c(j):
        finish(got(j, 3) + got(j, 4), 1 + 2 * core, j)

    @pl.when(core == 0)
    def _():
        pump(0, 1)
        m_first(0)
        pump(0, 2)
        e_second()
        pump(0, 1)
        m_first(1)
        pump(0, 2)
        m_second(0)
        pump(0, 1)
        up.wait_recv()
        turn(3, 2)
        pump(0, 1)
        s_first(0, 2, 2)
        s_first(1, 2, 2)
        pump(0, 1)
        m_first(2)
        m_second(1)
        s_first(2, 2, 2)
        s_second(0)
        s_second(1)
        m_first(3)
        s_first(3, 2, 2)
        m_second(2)
        s_second(2)
        e_third()
        for j in range(2):
            third_a(j)
            third_b(j)
        for j in range(4):
            third_c(j)
        s_second(3)
        m_second(3)

    @pl.when(core == 1)
    def _():
        pump(1, 1)
        s_first(0, 1, 0)
        s_first(1, 1, 0)
        pump(1, 2)
        s_first(2, 1, 0)
        s_first(3, 1, 0)
        pump(1, 2)
        e_second()
        m_first(0)
        pump(1, 1)
        s_second(0)
        s_second(1)
        pump(1, 1)
        s_second(2)
        s_second(3)
        pump(1, 2)
        m_first(1)
        pump(1, 1)
        m_second(0)
        pump(1, 3)
        m_first(2)
        m_second(1)
        e_third()
        for j in range(2):
            third_a(j)
            third_b(j)
        m_second(2)
        m_first(3)
        m_second(3)
        for j in range(4):
            third_c(j)

    for j in (2, 3):
        third_a(j)
        third_b(j)
    assert started == [16, 16]

    beside.wait_send()

    @pl.when(core == 1)
    def _():
        up.wait_send()

    for note in notes:
        note.wait_send()
    f_e.wait_send()
    for d in (1, 2, 3):
        y_e(d).wait_send()
    for i in range(12, 16):
        down(i).wait_send()
    for j in range(4):
        for d in (1, 2, 3):
            y_m(j, d).wait_send()
            y_s(j, d).wait_send()
        for i in range(5):
            f_l(j, i).wait_send()


def solution(mesh):
    parts, groups = mesh.shape["mesh"], mesh.shape["mem"]

    def per_device(x, coord, level):
        rows, width = x.shape
        owned = width // groups
        dma, vmem, i16 = pltpu.SemaphoreType.DMA, pltpu.VMEM, jnp.int16
        body = functools.partial(kernel, rows * groups, parts, 4.0 * width * parts, 12.0 * width)
        in_hbm = pl.BlockSpec(memory_space=pltpu.HBM)
        return pl.pallas_call(
            body,
            out_shape=jax.ShapeDtypeStruct((owned, 4 * width), F32),
            in_specs=[in_hbm] * 3,
            out_specs=pl.BlockSpec(memory_space=pltpu.VMEM),
            scratch_shapes=[
                vmem((1, width), jnp.int32),
                vmem((1, width), jnp.int32),
                vmem((4, rows, width), jnp.bfloat16),
                vmem((4, 3, LANES, rows), jnp.bfloat16),
                vmem((4, 2 * LANES, LANES), F32),
                vmem((3, 1, width), jnp.int32),
                vmem((2, 2, 64, LANES), F32),
                vmem((4, 4, 64, LANES), F32),
                vmem((4, LANES, LANES), F32),
                vmem((4, 3, LANES, LANES), F32),
                vmem((4, 64, LANES), F32),
                vmem((4, 64, LANES), F32),
                vmem((3, 2, 64, LANES), F32),
                vmem((3, 528, LANES), i16),
                vmem((3, 528, LANES), i16),
                vmem((4, 3, 272, LANES), i16),
                vmem((4, 3, 272, LANES), i16),
                vmem((4, 3, 144, LANES), i16),
                vmem((4, 3, 144, LANES), i16),
                vmem((272, LANES), i16),
                vmem((272, LANES), i16),
                vmem((4, 5, 80, LANES), i16),
                vmem((4, 5, 80, LANES), i16),
                dma, dma((2,)), dma((16,)), dma((16,)), dma, dma, dma, dma, dma((3,)), dma((3,)),
                dma((3,)), dma((3,)), dma((4, 3)), dma((4, 3)), dma((4, 3)), dma((4, 3)), dma, dma, dma((4, 5)), dma((4, 5)),
            ],
            compiler_params=pltpu.CompilerParams(
                collective_id=0, has_side_effects=True, vmem_limit_bytes=67043328
            ),
        )(x, coord.reshape(1, width), level.reshape(1, width))

    in_specs = (P("mem", "mesh"), P("mesh"), P("mesh"))
    out_specs = P(("mesh", "mem"), None)
    return jax.shard_map(per_device, mesh=mesh, in_specs=in_specs, out_specs=out_specs, check_vma=False)
```

```python
import functools

import jax
import jax.numpy as jnp
from jax import lax
from jax.experimental import pallas as pl
from jax.experimental.pallas import tpu as pltpu
from jax.sharding import PartitionSpec as P

MESH = pl.DeviceIdType.MESH
LANES = 128
STEPS = 32000.0
F32 = jnp.float32


def gc_taper(radius):
    r2 = radius * radius
    r3 = r2 * radius
    near = r3 * (0.625 + radius * (0.5 - 0.25 * radius)) - (5.0 / 3.0) * r2 + 1.0
    safe = jnp.maximum(radius, 1.0)
    s2 = safe * safe
    s3 = s2 * safe
    far = s3 * (0.625 + safe * (safe / 12.0 - 0.5)) + (5.0 / 3.0) * s2 - 5.0 * safe + 4.0 - 2.0 / (3.0 * safe)
    return jnp.where(radius <= 1.0, near, jnp.where(radius <= 2.0, far, 0.0))


def encode(blocks, store):
    top = functools.reduce(jnp.maximum, [jnp.max(jnp.abs(b), axis=0, keepdims=True) for b in blocks])
    power = jnp.ceil(jnp.log2(jnp.maximum(top, 1.2e-38)))
    half = jnp.floor(0.5 * power)
    one, two = jnp.exp2(-half), jnp.exp2(half - power) * STEPS
    at = 0
    for b in blocks:
        rows = b.shape[0]
        store(at, rows, jnp.round((b * one) * two).astype(jnp.int32).astype(jnp.int16))
        at += rows
    store(at, 16, jnp.broadcast_to(power, (16, LANES)).astype(jnp.int32).astype(jnp.int16))


def scale_of(ref, rows):
    power = ref[pl.ds(rows, 16), :].astype(jnp.int32).astype(F32)[0:1]
    half = jnp.floor(0.5 * power)
    return jnp.exp2(half), jnp.exp2(power - half) / STEPS


def decode(ref, at, rows, scale):
    return (ref[pl.ds(at, rows), :].astype(jnp.int32).astype(F32) * scale[0]) * scale[1]


def kernel(
    members, parts, period, reach,
    x_ref, coord_hbm, level_hbm, out_ref,
    coord_ref, level_ref, held, turned, begun, coords, rowv, weight, own_e, own_l, keep_e, keep_l, split,
    ysend_e, yrecv_e, ysend_m, yrecv_m, ysend_s, yrecv_s, fsend_e, frecv_e, fsend_l, frecv_l,
    own_sem, note_sem, zs, zr, bs, br, us, ur, cs, cr, yse, yre, ysm, yrm, yss, yrs, fse, fre, fsl, frl,
):
    p, m = lax.axis_index("mesh"), lax.axis_index("mem")
    core, y, h = lax.rem(p, 2), m // 2, lax.rem(m, 2)
    far = m + 1 - 2 * h
    sib = p + 1 - 2 * core

    def at(shift):
        return lax.rem(p + shift + parts, parts)

    def ring(d):
        return (p, lax.rem(m + 2 * d, 8))

    mine = [
        pltpu.make_async_copy(x_ref, held.at[0], own_sem),
        pltpu.make_async_copy(coord_hbm, coord_ref, note_sem.at[0]),
        pltpu.make_async_copy(level_hbm, level_ref, note_sem.at[1]),
    ]
    for copy in mine:
        copy.start()

    barrier = pltpu.get_barrier_semaphore()
    peers = [(at(s), m) for s in (-3, -2, -1, 1, 2, 3)] + [ring(d) for d in (1, 2, 3)]
    peers += [(p, far), (at(1), far), (at(-1), far)]
    for peer in peers:
        pl.semaphore_signal(barrier, inc=1, device_id=peer, device_id_type=MESH)
    pl.semaphore_wait(barrier, len(peers))

    def send(src, dst, ssem, rsem, to):
        return pltpu.make_async_remote_copy(
            src_ref=src, dst_ref=dst, send_sem=ssem, recv_sem=rsem, device_id=to, device_id_type=MESH
        )

    piece, started = members // 32, [0, 0]

    def columns(j):
        return pl.ds(pl.multiple_of(j * LANES, LANES), LANES)

    def down(i):
        c, r = pl.ds(i // 4 * LANES, LANES), pl.ds(i % 4 * piece, piece)
        return send(x_ref.at[r, c], held.at[2, r, c], zs.at[i], zr.at[i], (at(-2), m))

    def pump(who, count):
        for i in range(started[who], started[who] + count):
            if i >= 4:
                down(i - 4).wait_send()
            down(i).start()
        started[who] += count

    beside = send(x_ref, held.at[1], bs, br, (sib, m))
    up = send(x_ref, held.at[3], us, ur, (at(1), m))
    notes = [send(coord_hbm, coords.at[k], cs.at[k], cr.at[k], (at(-1 - k), m)) for k in range(3)]
    for note in notes:
        note.start()
    beside.start()

    @pl.when(core == 0)
    def _():
        pump(0, 4)

    @pl.when(core == 1)
    def _():
        up.start()
        pump(1, 3)

    for copy in mine:
        copy.wait()

    def turn(slot, to):
        def body(q, carry):
            turned[q, to] = held[slot, :, columns(q)].T
            return carry

        lax.fori_loop(0, 4, body, 0)

    turn(0, 0)

    def e_blocks(row):
        full = jnp.dot(turned[row, 0], held[0], preferred_element_type=F32)
        return [full[:, k * LANES : (k + 1) * LANES] for k in range(4)]

    def y_e(d):
        return send(ysend_e.at[d - 1], yrecv_e.at[d - 1], yse.at[d - 1], yre.at[d - 1], ring(d))

    for d in (2, 1, 3):

        def put(a, n, v, d=d):
            ysend_e[d - 1, pl.ds(a, n), :] = v

        encode(e_blocks(lax.rem(y + d, 4)), put)
        y_e(d).start()
    for k, b in enumerate(e_blocks(y)):
        own_e[k] = b

    @pl.when(core == 0)
    def _():
        pump(0, 3)

    @pl.when(core == 1)
    def _():
        pump(1, 1)

    def as_rows(ref):
        line = ref[0:1, columns(y)].astype(F32)
        return jnp.broadcast_to(line, (LANES, LANES)).T

    for k, ref in enumerate((coord_ref, level_ref)):
        v = as_rows(ref)
        rowv[k, 0] = v[0:64]
        rowv[k, 1] = v[64:128]
    row = rowv[0, h]
    limit = 0.05 * rowv[1, h]
    for note in notes:
        note.wait_recv()
    for s in range(4):
        for j in range(4):
            c = pl.ds(j * LANES, LANES)
            col = (coord_ref[0:1, c] if s == 0 else coords[s - 1, 0:1, c]).astype(F32)
            gap = col - row
            gap = jnp.where(gap < 0.0, gap + period, gap)
            dist = jnp.minimum(gap, period - gap)
            weight[s, j] = gc_taper(dist / reach) * (1.0 / (members - 1.0))

    def finish(value, s, j):
        c = weight[s, j] * value
        out_ref[:, pl.ds(pl.multiple_of((s * 4 + j) * LANES, LANES), LANES)] = c - jnp.clip(c, -limit, limit)

    beside.wait_recv()
    turn(1, 1)
    f_e = send(fsend_e, frecv_e, fse, fre, (p, far))

    def e_second():
        for d in (1, 2, 3):
            y_e(d).wait_recv()
        scales = [scale_of(yrecv_e.at[d], 512) for d in range(3)]
        theirs = []
        for k in range(4):
            total = own_e[k]
            for d in range(3):
                total = total + decode(yrecv_e.at[d], k * LANES, LANES, scales[d])
            split[0, 0] = total[0:64]
            split[0, 1] = total[64:128]
            keep_e[k] = split[0, h]
            theirs.append(split[0, 1 - h])

        def put(a, n, v):
            fsend_e[pl.ds(a, n), :] = v

        encode(theirs, put)
        f_e.start()

    def e_third():
        f_e.wait_recv()
        scale = scale_of(frecv_e, 256)
        for k in range(4):
            finish(keep_e[k] + decode(frecv_e, k * 64, 64, scale), 0, k)

    def y_m(j, d):
        return send(ysend_m.at[j, d - 1], yrecv_m.at[j, d - 1], ysm.at[j, d - 1], yrm.at[j, d - 1], ring(d))

    def y_s(j, d):
        return send(ysend_s.at[j, d - 1], yrecv_s.at[j, d - 1], yss.at[j, d - 1], yrs.at[j, d - 1], ring(d))

    depth = members // 8
    head = depth * 2 // 3

    def m_product(row, j, start, size):
        k = pl.ds(start, size)
        pair = turned[row, 0:2, :, k].reshape(2 * LANES, size)
        return jnp.dot(pair, held[2, k, pl.ds(j * LANES, LANES)], preferred_element_type=F32)

    def m_blocks(d, j):
        row = lax.rem(y + d, 4)
        if j < 3:
            both = m_product(row, j, 0, depth)
        else:
            both = begun[d] + m_product(row, j, head, depth - head)
        return [both[0:LANES], both[LANES:]]

    def m_first(j):
        for i in range(3):
            down(4 * j + i).wait_recv()
        if j == 3:
            for d in range(4):
                begun[d] = m_product(lax.rem(y + d, 4), j, 0, head)
        down(4 * j + 3).wait_recv()
        for d in (2, 1, 3):

            def put(a, n, v, d=d):
                ysend_m[j, d - 1, pl.ds(a, n), :] = v

            encode(m_blocks(d, j), put)
            y_m(j, d).start()
        for k, b in enumerate(m_blocks(0, j)):
            own_l[j, k] = b

    def s_first(j, left, right):
        rhs = held.at[right, :, pl.ds(j * LANES, LANES)]
        for d in (2, 1, 3):

            def put(a, n, v, d=d):
                ysend_s[j, d - 1, pl.ds(a, n), :] = v

            encode([jnp.dot(turned[lax.rem(y + d, 4), left], rhs[...], preferred_element_type=F32)], put)
            y_s(j, d).start()
        own_l[j, 2] = jnp.dot(turned[y, left], rhs[...], preferred_element_type=F32)

    goals = [(p, far), (sib, m), (sib, far), (at(-1), m), (at(-1), far)]

    def f_l(j, i):
        return send(fsend_l.at[j, i], frecv_l.at[j, i], fsl.at[j, i], frl.at[j, i], goals[i])

    def gathered(j, k, recv, at_row, scales):
        total = own_l[j, k]
        for d in range(3):
            total = total + decode(recv.at[j, d], at_row, LANES, scales[d])
        split[k, 0] = total[0:64]
        split[k, 1] = total[64:128]

    def forward(j, i, value):
        def put(a, n, v):
            fsend_l[j, i, pl.ds(a, n), :] = v

        encode([value], put)
        f_l(j, i).start()

    def m_second(j):
        for d in (1, 2, 3):
            y_m(j, d).wait_recv()
        scales = [scale_of(yrecv_m.at[j, d], 256) for d in range(3)]
        gathered(j, 0, yrecv_m, 0, scales)
        forward(j, 0, split[0, 1 - h])
        gathered(j, 1, yrecv_m, LANES, scales)
        forward(j, 2, split[1, 1 - h])
        forward(j, 1, split[1, h])
        keep_l[j] = split[0, h]

    def s_second(j):
        for d in (1, 2, 3):
            y_s(j, d).wait_recv()
        gathered(j, 2, yrecv_s, 0, [scale_of(yrecv_s.at[j, d], 128) for d in range(3)])
        forward(j, 4, split[2, 1 - h])
        forward(j, 3, split[2, h])

    def got(j, i):
        f_l(j, i).wait_recv()
        return decode(frecv_l.at[j, i], 0, 64, scale_of(frecv_l.at[j, i], 64))

    def third_a(j):
        finish(keep_l[j] + got(j, 0), 2, j)

    def third_b(j):
        finish(got(j, 1) + got(j, 2), 3 - 2 * core, j)

    def third_c(j):
        finish(got(j, 3) + got(j, 4), 1 + 2 * core, j)

    @pl.when(core == 0)
    def _():
        pump(0, 1)
        m_first(0)
        pump(0, 2)
        e_second()
        pump(0, 1)
        m_first(1)
        pump(0, 2)
        m_second(0)
        pump(0, 1)
        up.wait_recv()
        turn(3, 2)
        pump(0, 1)
        s_first(0, 2, 2)
        s_first(1, 2, 2)
        pump(0, 1)
        m_first(2)
        m_second(1)
        s_first(2, 2, 2)
        s_second(0)
        s_second(1)
        m_first(3)
        s_first(3, 2, 2)
        m_second(2)
        s_second(2)
        e_third()
        for j in range(2):
            third_a(j)
            third_b(j)
        for j in range(4):
            third_c(j)
        s_second(3)
        m_second(3)

    @pl.when(core == 1)
    def _():
        pump(1, 1)
        s_first(0, 1, 0)
        s_first(1, 1, 0)
        pump(1, 2)
        s_first(2, 1, 0)
        s_first(3, 1, 0)
        pump(1, 2)
        e_second()
        m_first(0)
        pump(1, 1)
        s_second(0)
        s_second(1)
        pump(1, 1)
        s_second(2)
        s_second(3)
        pump(1, 2)
        m_first(1)
        pump(1, 1)
        m_second(0)
        pump(1, 2)
        m_first(2)
        m_second(1)
        e_third()
        for j in range(2):
            third_a(j)
            third_b(j)
        m_second(2)
        m_first(3)
        m_second(3)
        for j in range(4):
            third_c(j)

    for j in (2, 3):
        third_a(j)
        third_b(j)
    assert started == [16, 16]

    beside.wait_send()

    @pl.when(core == 1)
    def _():
        up.wait_send()

    for note in notes:
        note.wait_send()
    f_e.wait_send()
    for d in (1, 2, 3):
        y_e(d).wait_send()
    for i in range(12, 16):
        down(i).wait_send()
    for j in range(4):
        for d in (1, 2, 3):
            y_m(j, d).wait_send()
            y_s(j, d).wait_send()
        for i in range(5):
            f_l(j, i).wait_send()


def solution(mesh):
    parts, groups = mesh.shape["mesh"], mesh.shape["mem"]

    def per_device(x, coord, level):
        rows, width = x.shape
        owned = width // groups
        dma, vmem, i16 = pltpu.SemaphoreType.DMA, pltpu.VMEM, jnp.int16
        body = functools.partial(kernel, rows * groups, parts, 4.0 * width * parts, 12.0 * width)
        in_hbm = pl.BlockSpec(memory_space=pltpu.HBM)
        return pl.pallas_call(
            body,
            out_shape=jax.ShapeDtypeStruct((owned, 4 * width), F32),
            in_specs=[in_hbm] * 3,
            out_specs=pl.BlockSpec(memory_space=pltpu.VMEM),
            scratch_shapes=[
                vmem((1, width), jnp.int32),
                vmem((1, width), jnp.int32),
                vmem((4, rows, width), jnp.bfloat16),
                vmem((4, 3, LANES, rows), jnp.bfloat16),
                vmem((4, 2 * LANES, LANES), F32),
                vmem((3, 1, width), jnp.int32),
                vmem((2, 2, 64, LANES), F32),
                vmem((4, 4, 64, LANES), F32),
                vmem((4, LANES, LANES), F32),
                vmem((4, 3, LANES, LANES), F32),
                vmem((4, 64, LANES), F32),
                vmem((4, 64, LANES), F32),
                vmem((3, 2, 64, LANES), F32),
                vmem((3, 528, LANES), i16),
                vmem((3, 528, LANES), i16),
                vmem((4, 3, 272, LANES), i16),
                vmem((4, 3, 272, LANES), i16),
                vmem((4, 3, 144, LANES), i16),
                vmem((4, 3, 144, LANES), i16),
                vmem((272, LANES), i16),
                vmem((272, LANES), i16),
                vmem((4, 5, 80, LANES), i16),
                vmem((4, 5, 80, LANES), i16),
                dma, dma((2,)), dma((16,)), dma((16,)), dma, dma, dma, dma, dma((3,)), dma((3,)),
                dma((3,)), dma((3,)), dma((4, 3)), dma((4, 3)), dma((4, 3)), dma((4, 3)), dma, dma, dma((4, 5)), dma((4, 5)),
            ],
            compiler_params=pltpu.CompilerParams(
                collective_id=0, has_side_effects=True, vmem_limit_bytes=67043328
            ),
        )(x, coord.reshape(1, width), level.reshape(1, width))

    in_specs = (P("mem", "mesh"), P("mesh"), P("mesh"))
    out_specs = P(("mesh", "mem"), None)
    return jax.shard_map(per_device, mesh=mesh, in_specs=in_specs, out_specs=out_specs, check_vma=False)
```

```python
import functools

import jax
import jax.numpy as jnp
from jax import lax
from jax.experimental import pallas as pl
from jax.experimental.pallas import tpu as pltpu
from jax.sharding import PartitionSpec as P

MESH = pl.DeviceIdType.MESH
LANES = 128
STEPS = 32000.0
F32 = jnp.float32


def gc_taper(radius):
    r2 = radius * radius
    r3 = r2 * radius
    near = r3 * (0.625 + radius * (0.5 - 0.25 * radius)) - (5.0 / 3.0) * r2 + 1.0
    safe = jnp.maximum(radius, 1.0)
    s2 = safe * safe
    s3 = s2 * safe
    far = s3 * (0.625 + safe * (safe / 12.0 - 0.5)) + (5.0 / 3.0) * s2 - 5.0 * safe + 4.0 - 2.0 / (3.0 * safe)
    return jnp.where(radius <= 1.0, near, jnp.where(radius <= 2.0, far, 0.0))


def encode(blocks, store):
    top = functools.reduce(jnp.maximum, [jnp.max(jnp.abs(b), axis=0, keepdims=True) for b in blocks])
    power = jnp.ceil(jnp.log2(jnp.maximum(top, 1.2e-38)))
    half = jnp.floor(0.5 * power)
    one, two = jnp.exp2(-half), jnp.exp2(half - power) * STEPS
    at = 0
    for b in blocks:
        rows = b.shape[0]
        store(at, rows, jnp.round((b * one) * two).astype(jnp.int32).astype(jnp.int16))
        at += rows
    store(at, 16, jnp.broadcast_to(power, (16, LANES)).astype(jnp.int32).astype(jnp.int16))


def scale_of(ref, rows):
    power = ref[pl.ds(rows, 16), :].astype(jnp.int32).astype(F32)[0:1]
    half = jnp.floor(0.5 * power)
    return jnp.exp2(half), jnp.exp2(power - half) / STEPS


def decode(ref, at, rows, scale):
    return (ref[pl.ds(at, rows), :].astype(jnp.int32).astype(F32) * scale[0]) * scale[1]


def kernel(
    members, parts, period, reach,
    x_ref, coord_hbm, level_hbm, out_ref,
    coord_ref, level_ref, held, turned, begun, coords, rowv, weight, own_e, own_l, keep_e, keep_l, split,
    ysend_e, yrecv_e, ysend_m, yrecv_m, ysend_s, yrecv_s, fsend_e, frecv_e, fsend_l, frecv_l,
    own_sem, note_sem, zs, zr, bs, br, us, ur, cs, cr, yse, yre, ysm, yrm, yss, yrs, fse, fre, fsl, frl,
):
    p, m = lax.axis_index("mesh"), lax.axis_index("mem")
    core, y, h = lax.rem(p, 2), m // 2, lax.rem(m, 2)
    far = m + 1 - 2 * h
    sib = p + 1 - 2 * core

    def at(shift):
        return lax.rem(p + shift + parts, parts)

    def ring(d):
        return (p, lax.rem(m + 2 * d, 8))

    mine = [
        pltpu.make_async_copy(x_ref, held.at[0], own_sem),
        pltpu.make_async_copy(coord_hbm, coord_ref, note_sem.at[0]),
        pltpu.make_async_copy(level_hbm, level_ref, note_sem.at[1]),
    ]
    for copy in mine:
        copy.start()

    barrier = pltpu.get_barrier_semaphore()
    peers = [(at(s), m) for s in (-3, -2, -1, 1, 2, 3)] + [ring(d) for d in (1, 2, 3)]
    peers += [(p, far), (at(1), far), (at(-1), far)]
    for peer in peers:
        pl.semaphore_signal(barrier, inc=1, device_id=peer, device_id_type=MESH)
    pl.semaphore_wait(barrier, len(peers))

    def send(src, dst, ssem, rsem, to):
        return pltpu.make_async_remote_copy(
            src_ref=src, dst_ref=dst, send_sem=ssem, recv_sem=rsem, device_id=to, device_id_type=MESH
        )

    piece, started = members // 32, [0, 0]

    def columns(j):
        return pl.ds(pl.multiple_of(j * LANES, LANES), LANES)

    def down(i):
        c, r = pl.ds(i // 4 * LANES, LANES), pl.ds(i % 4 * piece, piece)
        return send(x_ref.at[r, c], held.at[2, r, c], zs.at[i], zr.at[i], (at(-2), m))

    def pump(who, count):
        for i in range(started[who], started[who] + count):
            if i >= 4:
                down(i - 4).wait_send()
            down(i).start()
        started[who] += count

    beside = send(x_ref, held.at[1], bs, br, (sib, m))
    up = send(x_ref, held.at[3], us, ur, (at(1), m))
    notes = [send(coord_hbm, coords.at[k], cs.at[k], cr.at[k], (at(-1 - k), m)) for k in range(3)]
    for note in notes:
        note.start()
    beside.start()

    @pl.when(core == 0)
    def _():
        pump(0, 4)

    @pl.when(core == 1)
    def _():
        pump(1, 4)
        up.start()

    for copy in mine:
        copy.wait()

    def turn(slot, to):
        def body(q, carry):
            turned[q, to] = held[slot, :, columns(q)].T
            return carry

        lax.fori_loop(0, 4, body, 0)

    turn(0, 0)

    def e_blocks(row):
        full = jnp.dot(turned[row, 0], held[0], preferred_element_type=F32)
        return [full[:, k * LANES : (k + 1) * LANES] for k in range(4)]

    def y_e(d):
        return send(ysend_e.at[d - 1], yrecv_e.at[d - 1], yse.at[d - 1], yre.at[d - 1], ring(d))

    for d in (2, 1, 3):

        def put(a, n, v, d=d):
            ysend_e[d - 1, pl.ds(a, n), :] = v

        encode(e_blocks(lax.rem(y + d, 4)), put)
        y_e(d).start()
    for k, b in enumerate(e_blocks(y)):
        own_e[k] = b

    @pl.when(core == 0)
    def _():
        pump(0, 3)

    def as_rows(ref):
        line = ref[0:1, columns(y)].astype(F32)
        return jnp.broadcast_to(line, (LANES, LANES)).T

    for k, ref in enumerate((coord_ref, level_ref)):
        v = as_rows(ref)
        rowv[k, 0] = v[0:64]
        rowv[k, 1] = v[64:128]
    row = rowv[0, h]
    limit = 0.05 * rowv[1, h]
    for note in notes:
        note.wait_recv()
    for s in range(4):
        for j in range(4):
            c = pl.ds(j * LANES, LANES)
            col = (coord_ref[0:1, c] if s == 0 else coords[s - 1, 0:1, c]).astype(F32)
            gap = col - row
            gap = jnp.where(gap < 0.0, gap + period, gap)
            dist = jnp.minimum(gap, period - gap)
            weight[s, j] = gc_taper(dist / reach) * (1.0 / (members - 1.0))

    def finish(value, s, j):
        c = weight[s, j] * value
        out_ref[:, pl.ds(pl.multiple_of((s * 4 + j) * LANES, LANES), LANES)] = c - jnp.clip(c, -limit, limit)

    beside.wait_recv()
    turn(1, 1)
    f_e = send(fsend_e, frecv_e, fse, fre, (p, far))

    def e_second():
        for d in (1, 2, 3):
            y_e(d).wait_recv()
        scales = [scale_of(yrecv_e.at[d], 512) for d in range(3)]
        theirs = []
        for k in range(4):
            total = own_e[k]
            for d in range(3):
                total = total + decode(yrecv_e.at[d], k * LANES, LANES, scales[d])
            split[0, 0] = total[0:64]
            split[0, 1] = total[64:128]
            keep_e[k] = split[0, h]
            theirs.append(split[0, 1 - h])

        def put(a, n, v):
            fsend_e[pl.ds(a, n), :] = v

        encode(theirs, put)
        f_e.start()

    def e_third():
        f_e.wait_recv()
        scale = scale_of(frecv_e, 256)
        for k in range(4):
            finish(keep_e[k] + decode(frecv_e, k * 64, 64, scale), 0, k)

    def y_m(j, d):
        return send(ysend_m.at[j, d - 1], yrecv_m.at[j, d - 1], ysm.at[j, d - 1], yrm.at[j, d - 1], ring(d))

    def y_s(j, d):
        return send(ysend_s.at[j, d - 1], yrecv_s.at[j, d - 1], yss.at[j, d - 1], yrs.at[j, d - 1], ring(d))

    depth = members // 8
    head = depth * 2 // 3

    def m_product(row, j, start, size):
        k = pl.ds(start, size)
        pair = turned[row, 0:2, :, k].reshape(2 * LANES, size)
        return jnp.dot(pair, held[2, k, pl.ds(j * LANES, LANES)], preferred_element_type=F32)

    def m_blocks(d, j):
        row = lax.rem(y + d, 4)
        if j < 3:
            both = m_product(row, j, 0, depth)
        else:
            both = begun[d] + m_product(row, j, head, depth - head)
        return [both[0:LANES], both[LANES:]]

    def m_first(j):
        for i in range(3):
            down(4 * j + i).wait_recv()
        if j == 3:
            for d in range(4):
                begun[d] = m_product(lax.rem(y + d, 4), j, 0, head)
        down(4 * j + 3).wait_recv()
        for d in (2, 1, 3):

            def put(a, n, v, d=d):
                ysend_m[j, d - 1, pl.ds(a, n), :] = v

            encode(m_blocks(d, j), put)
            y_m(j, d).start()
        for k, b in enumerate(m_blocks(0, j)):
            own_l[j, k] = b

    def s_first(j, left, right):
        rhs = held.at[right, :, pl.ds(j * LANES, LANES)]
        for d in (2, 1, 3):

            def put(a, n, v, d=d):
                ysend_s[j, d - 1, pl.ds(a, n), :] = v

            encode([jnp.dot(turned[lax.rem(y + d, 4), left], rhs[...], preferred_element_type=F32)], put)
            y_s(j, d).start()
        own_l[j, 2] = jnp.dot(turned[y, left], rhs[...], preferred_element_type=F32)

    goals = [(p, far), (sib, m), (sib, far), (at(-1), m), (at(-1), far)]

    def f_l(j, i):
        return send(fsend_l.at[j, i], frecv_l.at[j, i], fsl.at[j, i], frl.at[j, i], goals[i])

    def gathered(j, k, recv, at_row, scales):
        total = own_l[j, k]
        for d in range(3):
            total = total + decode(recv.at[j, d], at_row, LANES, scales[d])
        split[k, 0] = total[0:64]
        split[k, 1] = total[64:128]

    def forward(j, i, value):
        def put(a, n, v):
            fsend_l[j, i, pl.ds(a, n), :] = v

        encode([value], put)
        f_l(j, i).start()

    def m_second(j):
        for d in (1, 2, 3):
            y_m(j, d).wait_recv()
        scales = [scale_of(yrecv_m.at[j, d], 256) for d in range(3)]
        gathered(j, 0, yrecv_m, 0, scales)
        forward(j, 0, split[0, 1 - h])
        gathered(j, 1, yrecv_m, LANES, scales)
        forward(j, 2, split[1, 1 - h])
        forward(j, 1, split[1, h])
        keep_l[j] = split[0, h]

    def s_second(j):
        for d in (1, 2, 3):
            y_s(j, d).wait_recv()
        gathered(j, 2, yrecv_s, 0, [scale_of(yrecv_s.at[j, d], 128) for d in range(3)])
        forward(j, 4, split[2, 1 - h])
        forward(j, 3, split[2, h])

    def got(j, i):
        f_l(j, i).wait_recv()
        return decode(frecv_l.at[j, i], 0, 64, scale_of(frecv_l.at[j, i], 64))

    def third_a(j):
        finish(keep_l[j] + got(j, 0), 2, j)

    def third_b(j):
        finish(got(j, 1) + got(j, 2), 3 - 2 * core, j)

    def third_c(j):
        finish(got(j, 3) + got(j, 4), 1 + 2 * core, j)

    @pl.when(core == 0)
    def _():
        pump(0, 1)
        m_first(0)
        pump(0, 2)
        e_second()
        pump(0, 1)
        m_first(1)
        pump(0, 2)
        m_second(0)
        pump(0, 1)
        up.wait_recv()
        turn(3, 2)
        pump(0, 1)
        s_first(0, 2, 2)
        s_first(1, 2, 2)
        pump(0, 1)
        m_first(2)
        m_second(1)
        s_first(2, 2, 2)
        s_second(0)
        s_second(1)
        m_first(3)
        s_first(3, 2, 2)
        m_second(2)
        s_second(2)
        e_third()
        for j in range(2):
            third_a(j)
            third_b(j)
        for j in range(4):
            third_c(j)
        s_second(3)
        m_second(3)

    @pl.when(core == 1)
    def _():
        pump(1, 1)
        s_first(0, 1, 0)
        s_first(1, 1, 0)
        pump(1, 2)
        s_first(2, 1, 0)
        s_first(3, 1, 0)
        pump(1, 2)
        e_second()
        m_first(0)
        pump(1, 1)
        s_second(0)
        s_second(1)
        pump(1, 1)
        s_second(2)
        s_second(3)
        pump(1, 2)
        m_first(1)
        pump(1, 1)
        m_second(0)
        pump(1, 2)
        m_first(2)
        m_second(1)
        e_third()
        for j in range(2):
            third_a(j)
            third_b(j)
        m_second(2)
        m_first(3)
        m_second(3)
        for j in range(4):
            third_c(j)

    for j in (2, 3):
        third_a(j)
        third_b(j)
    assert started == [16, 16]

    beside.wait_send()

    @pl.when(core == 1)
    def _():
        up.wait_send()

    for note in notes:
        note.wait_send()
    f_e.wait_send()
    for d in (1, 2, 3):
        y_e(d).wait_send()
    for i in range(12, 16):
        down(i).wait_send()
    for j in range(4):
        for d in (1, 2, 3):
            y_m(j, d).wait_send()
            y_s(j, d).wait_send()
        for i in range(5):
            f_l(j, i).wait_send()


def solution(mesh):
    parts, groups = mesh.shape["mesh"], mesh.shape["mem"]

    def per_device(x, coord, level):
        rows, width = x.shape
        owned = width // groups
        dma, vmem, i16 = pltpu.SemaphoreType.DMA, pltpu.VMEM, jnp.int16
        body = functools.partial(kernel, rows * groups, parts, 4.0 * width * parts, 12.0 * width)
        in_hbm = pl.BlockSpec(memory_space=pltpu.HBM)
        return pl.pallas_call(
            body,
            out_shape=jax.ShapeDtypeStruct((owned, 4 * width), F32),
            in_specs=[in_hbm] * 3,
            out_specs=pl.BlockSpec(memory_space=pltpu.VMEM),
            scratch_shapes=[
                vmem((1, width), jnp.int32),
                vmem((1, width), jnp.int32),
                vmem((4, rows, width), jnp.bfloat16),
                vmem((4, 3, LANES, rows), jnp.bfloat16),
                vmem((4, 2 * LANES, LANES), F32),
                vmem((3, 1, width), jnp.int32),
                vmem((2, 2, 64, LANES), F32),
                vmem((4, 4, 64, LANES), F32),
                vmem((4, LANES, LANES), F32),
                vmem((4, 3, LANES, LANES), F32),
                vmem((4, 64, LANES), F32),
                vmem((4, 64, LANES), F32),
                vmem((3, 2, 64, LANES), F32),
                vmem((3, 528, LANES), i16),
                vmem((3, 528, LANES), i16),
                vmem((4, 3, 272, LANES), i16),
                vmem((4, 3, 272, LANES), i16),
                vmem((4, 3, 144, LANES), i16),
                vmem((4, 3, 144, LANES), i16),
                vmem((272, LANES), i16),
                vmem((272, LANES), i16),
                vmem((4, 5, 80, LANES), i16),
                vmem((4, 5, 80, LANES), i16),
                dma, dma((2,)), dma((16,)), dma((16,)), dma, dma, dma, dma, dma((3,)), dma((3,)),
                dma((3,)), dma((3,)), dma((4, 3)), dma((4, 3)), dma((4, 3)), dma((4, 3)), dma, dma, dma((4, 5)), dma((4, 5)),
            ],
            compiler_params=pltpu.CompilerParams(
                collective_id=0, has_side_effects=True, vmem_limit_bytes=67043328
            ),
        )(x, coord.reshape(1, width), level.reshape(1, width))

    in_specs = (P("mem", "mesh"), P("mesh"), P("mesh"))
    out_specs = P(("mesh", "mem"), None)
    return jax.shard_map(per_device, mesh=mesh, in_specs=in_specs, out_specs=out_specs, check_vma=False)
```
